32 devices in a mesh: val: 4 (over x, core), cond: 8 (over z, y).
Axes of the slice: x: 2, y: 2, z: 4, core: 2. Of those that a mesh axis runs over, the one named last changes fastest.
Arguments:
- val_orbitals: bfloat16 [16, 768], P('val'), may hold values from -6 to 6
- cond_orbitals: bfloat16 [64, 768], P('cond'), may hold values from -6 to 6
- val_energy: bfloat16 [16], P('val'), may hold values from -0.59765625 to -0.049804688
- cond_energy: bfloat16 [64], P('cond'), may hold values from 0.049804688 to 1.1953125
- wave_index: int32 [4096], P('cond'), may hold values from 0 to 884735
Outputs:
- chi_real: float32 [128, 4096], P('val', 'cond')
- chi_imag: float32 [128, 4096], P('val', 'cond')
The draws below stay inside these ranges and needn't reach their ends.
Inputs may be any that keep to these rules, and one draw needn't show every extreme that they name: `wave_index`: values may repeat.
All inputs are finite; a program needn't handle non-finite values.
Results may differ from the reference program's by a relative error of at most 0.0037.
Values may be sent and summed in bfloat16 or wider, within the bound.
A program may use at most 64 MiB of HBM per device.

```python
import math
import jax
import jax.numpy as jnp
from jax import lax

NG = 96
NPW = 4096
NW = 128
SLAB_Y = 4
NPTS = 768
NVAL = 16
NCOND = 64


def set_ends(values, own_key, low, high):
    index_at = [jax.random.randint(jax.random.fold_in(own_key, axis), (), 0, length) for axis, length in enumerate(values.shape)]
    widest = values.shape.index(max(values.shape))
    next_to = index_at[:widest] + [(index_at[widest] + 1) % values.shape[widest]] + index_at[widest + 1:]
    return values.at[tuple(index_at)].set(low).at[tuple(next_to)].set(high)


def levels(rng, extent, pieces, low, largest):
    factor_of = 1.0
    for dim, shards_of in pieces:
        draws = jax.random.uniform(jax.random.fold_in(jax.random.fold_in(rng, 6), dim), (shards_of,), jnp.float32, low / len(pieces), largest / len(pieces))
        factor_of = factor_of * jnp.repeat(jnp.exp(draws), extent[dim] // shards_of).reshape((-1,) + (1,) * (len(extent) - 1 - dim))
    return factor_of


def bell_draw(key, shape, scale, limit, cuts=(), held_as=jnp.bfloat16):
    drawn = scale * jax.random.normal(key, shape, jnp.float32)
    if cuts:
        drawn = drawn * levels(key, shape, cuts, -0.22, 0.18)
    return jnp.clip(drawn, -limit, limit).astype(held_as)


def setup_inputs(seed: int = 0) -> dict:
    keys = jax.random.split(jax.random.key(seed), 6)
    return {
        "val_orbitals": bell_draw(keys[0], (NVAL, NPTS), 1.0, 6.0, ((0, 4),)),
        "cond_orbitals": bell_draw(keys[1], (NCOND, NPTS), 1.0, 6.0, ((0, 8),)),
        "val_energy": jnp.clip(-0.59765625 + 0.54785156 * jax.random.uniform(keys[2], (NVAL,), jnp.float32) ** levels(keys[2], (NVAL,), ((0, 4),), -0.2, 0.2), -0.59765625, -0.049804688).astype(jnp.bfloat16),
        "cond_energy": jnp.clip(0.049804688 + 1.1455078 * jax.random.uniform(keys[3], (NCOND,), jnp.float32) ** levels(keys[3], (NCOND,), ((0, 8),), -0.2, 0.2), 0.049804688, 1.1953125).astype(jnp.bfloat16),
        "wave_index": set_ends(jax.random.randint(keys[4], (NPW,), 0, NG * NG * NG), jax.random.fold_in(keys[4], 1), 0, (NG * NG * NG) - 1).astype(jnp.int32),
    }


def phase_table(wave_index, point_count, grid_cells, slab_rows):
    points = lax.iota(jnp.int32, point_count)
    along_x = points % grid_cells
    along_y = points // grid_cells % slab_rows
    along_z = points // (grid_cells * slab_rows)
    wave_x = wave_index // (grid_cells * grid_cells)
    wave_y = wave_index // grid_cells % grid_cells
    wave_z = wave_index % grid_cells
    phase_turns = (along_x[:, None] * wave_x[None, :] + along_y[:, None] * wave_y[None, :] + along_z[:, None] * wave_z[None, :]) % grid_cells
    angles = phase_turns.astype(jnp.float32) * (2.0 * math.pi / grid_cells)
    return jnp.concatenate([jnp.cos(angles), jnp.sin(angles)], axis=1).astype(jnp.bfloat16)

def reference(val_orbitals, cond_orbitals, val_energy, cond_energy, wave_index):
    row_table = phase_table(wave_index, NPTS, NG, SLAB_Y)
    window_table = phase_table(wave_index[:NW], NPTS, NG, SLAB_Y)
    cond_energies = cond_energy.astype(jnp.float32)
    cond_values = cond_orbitals.astype(jnp.float32)

    def one_valence(totals, inputs):
        orbital, energy = inputs
        density = (cond_values * orbital[None, :].astype(jnp.float32)).astype(jnp.bfloat16)
        window_terms = jnp.dot(density, window_table, preferred_element_type=jnp.float32)
        weights = 1.0 / (cond_energies - energy.astype(jnp.float32))
        weighted = window_terms * weights[:, None]
        update = jnp.dot(weighted.T, density.astype(jnp.float32), precision=lax.Precision.HIGHEST)
        return (totals + update, None)
    totals, unused = lax.scan(one_valence, jnp.zeros((2 * NW, NPTS), jnp.float32), (val_orbitals, val_energy))
    products = jnp.dot(totals, row_table.astype(jnp.float32), precision=lax.Precision.HIGHEST)
    factor = -4.0 / math.sqrt(NVAL * NCOND)
    real_part = factor * (products[:NW, :NPW] + products[NW:, NPW:])
    imag_part = factor * (products[:NW, NPW:] - products[NW:, :NPW])
    return (real_part, imag_part)
```

```python
import functools
import math

import jax
import jax.numpy as jnp
from jax import lax
from jax.experimental import pallas as pl
from jax.experimental.pallas import tpu as pltpu
from jax.sharding import PartitionSpec as P

NG = 96
NW = 128
SLAB_Y = 4
LANES = 128
MESH = pl.DeviceIdType.MESH


def modulo(value, period):
    return value - period * jnp.floor((value + 0.5) * (1.0 / period))


def cos_turns(turns):
    angle = (turns - NG / 2) * (math.pi / NG)
    square = angle * angle
    series = 1.0
    for order in (10, 8, 6, 4, 2):
        series = 1.0 - square * series * (1.0 / (order * (order + 1)))
    sine = angle * series
    return 2.0 * sine * sine - 1.0


def wave_parts(index):
    flat = index.astype(jnp.float32)
    wave_x = jnp.floor((flat + 0.5) * (1.0 / (NG * NG)))
    rest = flat - wave_x * (NG * NG)
    wave_y = jnp.floor((rest + 0.5) * (1.0 / NG))
    return wave_x, wave_y, rest - wave_y * NG


def factors(index, points, shift):
    wave_x, wave_y, wave_z = wave_parts(index)
    planes = points // NG
    along_x = lax.broadcasted_iota(jnp.int32, (NG, LANES), 0).astype(jnp.float32)
    plane = lax.broadcasted_iota(jnp.int32, (planes, LANES), 0).astype(jnp.float32)
    along_z = jnp.floor((plane + 0.5) * (1.0 / SLAB_Y))
    along_y = plane - along_z * SLAB_Y
    turns_x = modulo(along_x * wave_x, NG)
    turns_yz = modulo(along_y * wave_y + along_z * wave_z + shift, NG)
    quarter = 3 * NG // 4
    return (
        cos_turns(turns_x),
        cos_turns(modulo(turns_x + quarter, NG)),
        cos_turns(turns_yz),
        cos_turns(modulo(turns_yz + quarter, NG)),
    )


def split(value):
    high = value.astype(jnp.bfloat16)
    low = (value - high.astype(jnp.float32)).astype(jnp.bfloat16)
    return jnp.concatenate([high, low], axis=0)


def dot(left, right):
    return jnp.dot(left, right, preferred_element_type=jnp.float32)


def kernel(
    nv, nc, vb, cb, points,
    packed, wave, real, imag,
    gath_v, gath_c, own_wave, window, cos_rows, sin_rows, window_table, dens, totals,
    send_v, recv_v, send_c, recv_c, send_w, recv_w, local,
):
    iv = lax.axis_index("val")
    ic = lax.axis_index("cond")
    rows = NW // nv
    planes = points // NG

    barrier = pltpu.get_barrier_semaphore()
    for d in range(1, nc):
        pl.semaphore_signal(barrier, inc=1, device_id={"cond": lax.rem(ic + d, nc)}, device_id_type=MESH)
    for d in range(1, nv):
        pl.semaphore_signal(barrier, inc=1, device_id={"val": lax.rem(iv + d, nv)}, device_id_type=MESH)

    wave_copy = pltpu.make_async_copy(wave, own_wave, local.at[0])
    cond_copy = pltpu.make_async_copy(packed.at[0], gath_c.at[ic], local.at[1])
    val_copy = pltpu.make_async_copy(packed.at[1], gath_v.at[iv], local.at[2])
    wave_copy.start()
    cond_copy.start()
    val_copy.start()
    wave_copy.wait()

    for block in range(own_wave.shape[0]):
        cos_x, sin_x, cos_p, sin_p = factors(own_wave[pl.ds(block, 1), :], points, 0.0)
        lanes = pl.ds(block * LANES, LANES)
        for plane in range(planes):
            at = pl.ds(plane * NG, NG)
            c, s = cos_p[plane:plane + 1, :], sin_p[plane:plane + 1, :]
            cos_rows[at, lanes] = (cos_x * c - sin_x * s).astype(jnp.bfloat16)
            sin_rows[at, lanes] = (sin_x * c + cos_x * s).astype(jnp.bfloat16)

    pl.semaphore_wait(barrier, nc - 1 + nv - 1)

    def window_copy(d):
        return pltpu.make_async_remote_copy(
            src_ref=wave.at[pl.ds(0, 1)], dst_ref=window,
            send_sem=send_w.at[d - 1], recv_sem=recv_w,
            device_id={"cond": lax.rem(ic + d, nc)}, device_id_type=MESH,
        )

    @pl.when(ic == 0)
    def _():
        for d in range(1, nc):
            window_copy(d).start()
        pltpu.make_async_copy(wave.at[pl.ds(0, 1)], window, local.at[3]).start()

    def cond_send(d):
        return pltpu.make_async_remote_copy(
            src_ref=packed.at[0], dst_ref=gath_c.at[ic],
            send_sem=send_c.at[d - 1], recv_sem=recv_c.at[d - 1],
            device_id={"cond": lax.rem(ic + d, nc)}, device_id_type=MESH,
        )

    def cond_recv(d):
        return pltpu.make_async_remote_copy(
            src_ref=packed.at[0], dst_ref=gath_c.at[lax.rem(ic + nc - d, nc)],
            send_sem=send_c.at[d - 1], recv_sem=recv_c.at[d - 1],
            device_id={"cond": lax.rem(ic + d, nc)}, device_id_type=MESH,
        )

    def val_send(d):
        return pltpu.make_async_remote_copy(
            src_ref=packed.at[1], dst_ref=gath_v.at[iv],
            send_sem=send_v.at[d - 1], recv_sem=recv_v.at[d - 1],
            device_id={"val": lax.rem(iv + d, nv)}, device_id_type=MESH,
        )

    def val_recv(d):
        return pltpu.make_async_remote_copy(
            src_ref=packed.at[1], dst_ref=gath_v.at[lax.rem(iv + nv - d, nv)],
            send_sem=send_v.at[d - 1], recv_sem=recv_v.at[d - 1],
            device_id={"val": lax.rem(iv + d, nv)}, device_id_type=MESH,
        )

    for d in range(1, nc):
        cond_send(d).start()
    for d in range(1, nv):
        val_send(d).start()

    @pl.when(ic == 0)
    def _():
        pltpu.make_async_copy(wave.at[pl.ds(0, 1)], window, local.at[3]).wait()

    @pl.when(ic != 0)
    def _():
        window_copy(1).wait_recv()

    spread = jnp.broadcast_to(window[...], (8, LANES))
    first = pltpu.roll(spread, lax.rem(NW - iv * rows, NW), 1)
    lane = lax.broadcasted_iota(jnp.int32, (8, LANES), 1)
    index = jnp.where(lane < rows, first, pltpu.roll(first, rows, 1))[0:1, :]
    shift = jnp.where(lane < rows, 0.0, 3 * NG / 4)[0:1, :]
    cos_x, sin_x, cos_p, sin_p = factors(index, points, shift)
    for plane in range(planes):
        c, s = cos_p[plane:plane + 1, :], sin_p[plane:plane + 1, :]
        window_table[pl.ds(plane * NG, NG), :] = (cos_x * c - sin_x * s).astype(jnp.bfloat16)

    val_copy.wait()
    cond_copy.wait()
    for d in range(1, nv):
        val_recv(d).wait_recv()
    for d in range(1, nc):
        cond_recv(d).wait_recv()

    count = nc * cb
    per_step = max(1, min(nv, 1024 // (count * vb)))
    totals[...] = jnp.zeros_like(totals)

    @pl.loop(0, nv // per_step)
    def _(step):
        cond = gath_c[:, 0:cb, 0:points].astype(jnp.float32).reshape(count, points)
        cond_energy = gath_c[:, 0:cb, points:points + LANES].astype(jnp.float32).reshape(count, LANES)
        weights = []
        for inner in range(per_step):
            block = gath_v[step * per_step + inner].astype(jnp.float32)
            for v in range(vb):
                at = pl.ds((inner * vb + v) * count, count)
                dens[at, :] = (cond * block[v:v + 1, 0:points]).astype(jnp.bfloat16)
                weights.append(1.0 / (cond_energy - block[v:v + 1, points:points + LANES]))
        weighted = dot(dens[...], window_table[...]) * jnp.concatenate(weights, axis=0)
        parts = split(jnp.transpose(weighted)[0:2 * rows])
        update = dot(parts, dens[...])
        totals[...] += update[0:2 * rows] + update[2 * rows:4 * rows]

    cos_total = totals[0:rows, :]
    sin_total = totals[rows:2 * rows, :]
    by_cos = split(jnp.concatenate([cos_total, -sin_total], axis=0))
    by_sin = split(jnp.concatenate([sin_total, cos_total], axis=0))
    both = dot(by_cos, cos_rows[...]) + dot(by_sin, sin_rows[...])
    factor = -4.0 / math.sqrt(nv * vb * count)
    both = factor * (both[0:2 * rows] + both[2 * rows:4 * rows])
    real[...] = both[0:rows]
    imag[...] = both[rows:2 * rows]

    @pl.when(ic == 0)
    def _():
        for d in range(1, nc):
            window_copy(d).wait_send()

    for d in range(1, nc):
        cond_send(d).wait_send()
    for d in range(1, nv):
        val_send(d).wait_send()


def per_device(val_orbitals, cond_orbitals, val_energy, cond_energy, wave_index):
    nv, nc = lax.axis_size("val"), lax.axis_size("cond")
    vb, points = val_orbitals.shape
    cb = cond_orbitals.shape[0]
    held = -(-max(vb, cb) // 8) * 8
    count = wave_index.shape[0]
    rows = NW // nv

    def pack(orbitals, energy):
        wide = jnp.broadcast_to(energy[:, None], (energy.shape[0], LANES))
        both = jnp.concatenate([orbitals, wide], axis=1)
        return jnp.pad(both, ((0, held - both.shape[0]), (0, 0)))

    packed = jnp.stack([pack(cond_orbitals, cond_energy), pack(val_orbitals, val_energy)])
    wave = wave_index.reshape(count // LANES, LANES)
    width = points + LANES
    pairs = max(1, min(nv, 1024 // (nc * cb * vb))) * vb * nc * cb
    shape = jax.ShapeDtypeStruct((rows, count), jnp.float32)
    return pl.pallas_call(
        functools.partial(kernel, nv, nc, vb, cb, points),
        out_shape=(shape, shape),
        in_specs=[pl.BlockSpec(memory_space=pl.ANY)] * 2,
        out_specs=[pl.BlockSpec(memory_space=pltpu.VMEM)] * 2,
        scratch_shapes=[
            pltpu.VMEM((nv, held, width), jnp.bfloat16),
            pltpu.VMEM((nc, held, width), jnp.bfloat16),
            pltpu.VMEM((count // LANES, LANES), jnp.int32),
            pltpu.VMEM((1, LANES), jnp.int32),
            pltpu.VMEM((points, count), jnp.bfloat16),
            pltpu.VMEM((points, count), jnp.bfloat16),
            pltpu.VMEM((points, LANES), jnp.bfloat16),
            pltpu.VMEM((pairs, points), jnp.bfloat16),
            pltpu.VMEM((2 * rows, points), jnp.float32),
            pltpu.SemaphoreType.DMA((nv - 1,)),
            pltpu.SemaphoreType.DMA((nv - 1,)),
            pltpu.SemaphoreType.DMA((nc - 1,)),
            pltpu.SemaphoreType.DMA((nc - 1,)),
            pltpu.SemaphoreType.DMA((nc - 1,)),
            pltpu.SemaphoreType.DMA,
            pltpu.SemaphoreType.DMA((4,)),
        ],
        compiler_params=pltpu.CompilerParams(collective_id=0, has_side_effects=True),
    )(packed, wave)


def solution(mesh):
    return jax.shard_map(
        per_device,
        mesh=mesh,
        in_specs=(P("val", None), P("cond", None), P("val"), P("cond"), P("cond")),
        out_specs=(P("val", "cond"), P("val", "cond")),
        check_vma=False,
    )
```

```python
import functools
import math

import jax
import jax.numpy as jnp
from jax import lax
from jax.experimental import pallas as pl
from jax.experimental.pallas import tpu as pltpu
from jax.sharding import PartitionSpec as P

NG = 96
NW = 128
SLAB_Y = 4
LANES = 128
VMEM_LIMIT = 24 * 1024 * 1024
MESH = pl.DeviceIdType.MESH


def modulo(value, period):
    return value - period * jnp.floor((value + 0.5) * (1.0 / period))


def cos_turns(turns):
    angle = (turns - NG / 2) * (math.pi / NG)
    square = angle * angle
    series = 1.0
    for order in (10, 8, 6, 4, 2):
        series = 1.0 - square * series * (1.0 / (order * (order + 1)))
    sine = angle * series
    return 2.0 * sine * sine - 1.0


def wave_parts(index):
    flat = index.astype(jnp.float32)
    wave_x = jnp.floor((flat + 0.5) * (1.0 / (NG * NG)))
    rest = flat - wave_x * (NG * NG)
    wave_y = jnp.floor((rest + 0.5) * (1.0 / NG))
    return wave_x, wave_y, rest - wave_y * NG


def factors(index, points, shift):
    wave_x, wave_y, wave_z = wave_parts(index)
    planes = points // NG
    along_x = lax.broadcasted_iota(jnp.int32, (NG, LANES), 0).astype(jnp.float32)
    plane = lax.broadcasted_iota(jnp.int32, (planes, LANES), 0).astype(jnp.float32)
    along_z = jnp.floor((plane + 0.5) * (1.0 / SLAB_Y))
    along_y = plane - along_z * SLAB_Y
    turns_x = modulo(along_x * wave_x, NG)
    turns_yz = modulo(along_y * wave_y + along_z * wave_z + shift, NG)
    quarter = 3 * NG // 4
    return (
        cos_turns(turns_x),
        cos_turns(modulo(turns_x + quarter, NG)),
        cos_turns(turns_yz),
        cos_turns(modulo(turns_yz + quarter, NG)),
    )


def split(value):
    high = value.astype(jnp.bfloat16)
    low = (value - high.astype(jnp.float32)).astype(jnp.bfloat16)
    return jnp.concatenate([high, low], axis=0)


def dot(left, right):
    return jnp.dot(left, right, preferred_element_type=jnp.float32)


def partner(position, offset, size):
    if size & (size - 1):
        return lax.rem(position + offset, size)
    bit = 1
    while bit < size:
        if offset & bit:
            position = position + bit - 2 * bit * lax.rem(position // bit, 2)
        bit *= 2
    return position


def source(position, offset, size):
    if size & (size - 1):
        return lax.rem(position + size - offset, size)
    return partner(position, offset, size)


def kernel(
    nv, nc, group, slots,
    val, cond, val_energy, cond_energy, wave, out,
    gath_v, gath_c, gath_ve, gath_ce, own_wave, window, cos_rows, sin_rows, window_table, dens, totals,
    send_v, recv_v, send_c, recv_c, send_ve, recv_ve, send_ce, recv_ce, send_w, recv_w, local,
):
    iv = lax.axis_index("val")
    ic = lax.axis_index("cond")
    vb, points = val.shape
    cb = cond.shape[0]
    rows = NW // nv
    planes = points // NG

    barrier = pltpu.get_barrier_semaphore()
    for d in range(nc - 1, 0, -1):
        pl.semaphore_signal(barrier, inc=1, device_id={"cond": partner(ic, d, nc)}, device_id_type=MESH)
    for d in range(1, nv):
        pl.semaphore_signal(barrier, inc=1, device_id={"val": partner(iv, d, nv)}, device_id_type=MESH)

    wave_copy = pltpu.make_async_copy(wave, own_wave, local.at[0])
    own_copies = [
        pltpu.make_async_copy(val, gath_v.at[iv], local.at[1]),
        pltpu.make_async_copy(val_energy, gath_ve.at[iv], local.at[2]),
        pltpu.make_async_copy(cond, gath_c.at[ic], local.at[3]),
        pltpu.make_async_copy(cond_energy, gath_ce.at[ic], local.at[4]),
    ]
    wave_copy.start()
    for copy in own_copies:
        copy.start()
    wave_copy.wait()

    for block in range(own_wave.shape[0]):
        cos_x, sin_x, cos_p, sin_p = factors(own_wave[pl.ds(block, 1), :], points, 0.0)
        lanes = pl.ds(block * LANES, LANES)
        for plane in range(planes):
            at = pl.ds(plane * NG, NG)
            c, s = cos_p[plane:plane + 1, :], sin_p[plane:plane + 1, :]
            cos_rows[at, lanes] = (cos_x * c - sin_x * s).astype(jnp.bfloat16)
            sin_rows[at, lanes] = (sin_x * c + cos_x * s).astype(jnp.bfloat16)

    pl.semaphore_wait(barrier, nc - 1 + nv - 1)

    def window_copy(d):
        return pltpu.make_async_remote_copy(
            src_ref=wave.at[pl.ds(0, 1)], dst_ref=window,
            send_sem=send_w.at[d - 1], recv_sem=recv_w,
            device_id={"cond": partner(ic, d, nc)}, device_id_type=MESH,
        )

    own_window = pltpu.make_async_copy(wave.at[pl.ds(0, 1)], window, local.at[5])

    @pl.when(ic == 0)
    def _():
        for d in range(nc - 1, 0, -1):
            window_copy(d).start()
        own_window.start()

    def exchange(axis, position, size, d, at, src, dst, send, recv):
        return pltpu.make_async_remote_copy(
            src_ref=src, dst_ref=dst.at[at],
            send_sem=send.at[d - 1], recv_sem=recv.at[d - 1],
            device_id={axis: partner(position, d, size)}, device_id_type=MESH,
        )

    def val_copies(d, at):
        return [
            exchange("val", iv, nv, d, at, val, gath_v, send_v, recv_v),
            exchange("val", iv, nv, d, at, val_energy, gath_ve, send_ve, recv_ve),
        ]

    def cond_copies(d, at):
        return [
            exchange("cond", ic, nc, d, at, cond, gath_c, send_c, recv_c),
            exchange("cond", ic, nc, d, at, cond_energy, gath_ce, send_ce, recv_ce),
        ]

    for d in range(nc - 1, 0, -1):
        for copy in cond_copies(d, ic):
            copy.start()
    for d in range(1, nv):
        for copy in val_copies(d, iv):
            copy.start()

    for copy in own_copies:
        copy.wait()
    for d in range(1, nv):
        for copy in val_copies(d, source(iv, d, nv)):
            copy.wait_recv()

    count = group * cb
    height = nv * vb * count
    eye = lax.broadcasted_iota(jnp.int32, (cb, cb), 0) == lax.broadcasted_iota(jnp.int32, (cb, cb), 1)

    def fill(first):
        slot = first // group % slots
        orbitals, energies = [], []
        for d in range(first, first + group):
            at = source(ic, d, nc) if d else ic
            if d:
                for copy in cond_copies(d, at):
                    copy.wait_recv()
            orbitals.append(gath_c[at].astype(jnp.float32))
            row = jnp.broadcast_to(gath_ce[at].astype(jnp.float32), (cb, cb))
            column = jnp.sum(jnp.where(eye, row, 0.0), axis=1, keepdims=True)
            energies.append(jnp.broadcast_to(column, (cb, LANES)))
        orbitals = jnp.concatenate(orbitals, axis=0)

        def one_block(b, carry):
            block = gath_v[b].astype(jnp.float32)
            for v in range(vb):
                at = pl.ds(pl.multiple_of((b * vb + v) * count, count), count)
                dens[slot, at, :] = (orbitals * block[v:v + 1, :]).astype(jnp.bfloat16)
            return carry

        lax.fori_loop(0, nv, one_block, 0, unroll=nv <= 4)
        return jnp.concatenate(energies, axis=0)

    def use(first, energies):
        slot = first // group % slots
        weights = []
        for b in range(nv):
            block = gath_ve[b].astype(jnp.float32)
            for v in range(vb):
                own = jnp.broadcast_to(block[:, v:v + 1], (1, LANES))
                weights.append(1.0 / (energies - own))
        weighted = dot(dens[slot], window_table[...]) * jnp.concatenate(weights, axis=0)
        update = dot(split(jnp.transpose(weighted)[0:2 * rows]), dens[slot])
        update = update[0:2 * rows] + update[2 * rows:4 * rows]
        totals[...] = update if first == 0 else totals[...] + update

    ahead = min(2, slots, nc // group)
    energies = {}
    for step in range(ahead):
        energies[step] = fill(step * group)

    @pl.when(ic == 0)
    def _():
        own_window.wait()

    @pl.when(ic != 0)
    def _():
        window_copy(1).wait_recv()

    spread = jnp.broadcast_to(window[...], (8, LANES))
    first = pltpu.roll(spread, lax.rem(NW - iv * rows, NW), 1)
    lane = lax.broadcasted_iota(jnp.int32, (8, LANES), 1)
    index = jnp.where(lane < rows, first, pltpu.roll(first, rows, 1))[0:1, :]
    shift = jnp.where(lane < rows, 0.0, 3 * NG / 4)[0:1, :]
    cos_x, sin_x, cos_p, sin_p = factors(index, points, shift)
    for plane in range(planes):
        c, s = cos_p[plane:plane + 1, :], sin_p[plane:plane + 1, :]
        window_table[pl.ds(plane * NG, NG), :] = (cos_x * c - sin_x * s).astype(jnp.bfloat16)

    for step in range(nc // group):
        if step >= ahead:
            energies[step] = fill(step * group)
        use(step * group, energies.pop(step))

    cos_total = totals[0:rows, :]
    sin_total = totals[rows:2 * rows, :]
    by_cos = split(jnp.concatenate([cos_total, -sin_total], axis=0))
    by_sin = split(jnp.concatenate([sin_total, cos_total], axis=0))
    both = dot(by_cos, cos_rows[...]) + dot(by_sin, sin_rows[...])
    out[...] = both[0:2 * rows] + both[2 * rows:4 * rows]

    @pl.when(ic == 0)
    def _():
        for d in range(1, nc):
            window_copy(d).wait_send()

    for d in range(1, nc):
        for copy in cond_copies(d, ic):
            copy.wait_send()
    for d in range(1, nv):
        for copy in val_copies(d, iv):
            copy.wait_send()


def per_device(val_orbitals, cond_orbitals, val_energy, cond_energy, wave_index):
    nv, nc = lax.axis_size("val"), lax.axis_size("cond")
    vb, points = val_orbitals.shape
    cb = cond_orbitals.shape[0]
    count = wave_index.shape[0]
    rows = NW // nv
    group = 2 if nc % 2 == 0 else 1
    slots = min(4, nc // group)
    bf16, f32 = jnp.bfloat16, jnp.float32
    dma = pltpu.SemaphoreType.DMA
    out = pl.pallas_call(
        functools.partial(kernel, nv, nc, group, slots),
        out_shape=jax.ShapeDtypeStruct((2 * rows, count), f32),
        in_specs=[pl.BlockSpec(memory_space=pltpu.HBM)] * 5,
        out_specs=pl.BlockSpec(memory_space=pltpu.VMEM),
        scratch_shapes=[
            pltpu.VMEM((nv, vb, points), bf16),
            pltpu.VMEM((nc, cb, points), bf16),
            pltpu.VMEM((nv, 1, vb), bf16),
            pltpu.VMEM((nc, 1, cb), bf16),
            pltpu.VMEM((count // LANES, LANES), jnp.int32),
            pltpu.VMEM((1, LANES), jnp.int32),
            pltpu.VMEM((points, count), bf16),
            pltpu.VMEM((points, count), bf16),
            pltpu.VMEM((points, LANES), bf16),
            pltpu.VMEM((slots, nv * vb * group * cb, points), bf16),
            pltpu.VMEM((2 * rows, points), f32),
            dma((nv - 1,)), dma((nv - 1,)), dma((nc - 1,)), dma((nc - 1,)),
            dma((nv - 1,)), dma((nv - 1,)), dma((nc - 1,)), dma((nc - 1,)),
            dma((nc - 1,)), dma, dma((6,)),
        ],
        compiler_params=pltpu.CompilerParams(
            collective_id=0, has_side_effects=True, vmem_limit_bytes=VMEM_LIMIT
        ),
    )(*[
        pltpu.with_memory_space_constraint(value, pltpu.HBM)
        for value in (
            val_orbitals, cond_orbitals, val_energy.reshape(1, vb), cond_energy.reshape(1, cb),
            wave_index.reshape(count // LANES, LANES),
        )
    ])
    factor = -4.0 / math.sqrt(nv * vb * nc * cb)
    return factor * out[0:rows], factor * out[rows:2 * rows]


def solution(mesh):
    return jax.shard_map(
        per_device,
        mesh=mesh,
        in_specs=(P("val", None), P("cond", None), P("val"), P("cond"), P("cond")),
        out_specs=(P("val", "cond"), P("val", "cond")),
        check_vma=False,
    )
```

```python
import functools
import math

import jax
import jax.numpy as jnp
from jax import lax
from jax.experimental import pallas as pl
from jax.experimental.pallas import tpu as pltpu
from jax.sharding import PartitionSpec as P

NG = 96
NW = 128
SLAB_Y = 4
LANES = 128
VMEM_LIMIT = 24 * 1024 * 1024
MESH = pl.DeviceIdType.MESH


def modulo(value, period):
    return value - period * jnp.floor((value + 0.5) * (1.0 / period))


def cos_turns(turns):
    angle = (turns - NG / 2) * (math.pi / NG)
    square = angle * angle
    series = 1.0
    for order in (10, 8, 6, 4, 2):
        series = 1.0 - square * series * (1.0 / (order * (order + 1)))
    sine = angle * series
    return 2.0 * sine * sine - 1.0


def wave_parts(index):
    flat = index.astype(jnp.float32)
    wave_x = jnp.floor((flat + 0.5) * (1.0 / (NG * NG)))
    rest = flat - wave_x * (NG * NG)
    wave_y = jnp.floor((rest + 0.5) * (1.0 / NG))
    return wave_x, wave_y, rest - wave_y * NG


def factors(index, points, shift):
    wave_x, wave_y, wave_z = wave_parts(index)
    planes = points // NG
    along_x = lax.broadcasted_iota(jnp.int32, (NG, LANES), 0).astype(jnp.float32)
    plane = lax.broadcasted_iota(jnp.int32, (planes, LANES), 0).astype(jnp.float32)
    along_z = jnp.floor((plane + 0.5) * (1.0 / SLAB_Y))
    along_y = plane - along_z * SLAB_Y
    turns_x = modulo(along_x * wave_x, NG)
    turns_yz = modulo(along_y * wave_y + along_z * wave_z + shift, NG)
    quarter = 3 * NG // 4
    return (
        cos_turns(turns_x),
        cos_turns(modulo(turns_x + quarter, NG)),
        cos_turns(turns_yz),
        cos_turns(modulo(turns_yz + quarter, NG)),
    )


def split(value):
    high = value.astype(jnp.bfloat16)
    low = (value - high.astype(jnp.float32)).astype(jnp.bfloat16)
    return jnp.concatenate([high, low], axis=0)


def dot(left, right):
    return jnp.dot(left, right, preferred_element_type=jnp.float32)


def partner(position, offset, size):
    if size & (size - 1):
        return lax.rem(position + offset, size)
    bit = 1
    while bit < size:
        if offset & bit:
            position = position + bit - 2 * bit * lax.rem(position // bit, 2)
        bit *= 2
    return position


def source(position, offset, size):
    if size & (size - 1):
        return lax.rem(position + size - offset, size)
    return partner(position, offset, size)


def kernel(
    nv, nc, group, slots,
    val, cond, val_energy, cond_energy, wave, out,
    gath_v, gath_c, gath_ve, gath_ce, own_wave, window, cos_rows, sin_rows, window_table, dens, totals,
    send_v, recv_v, send_c, recv_c, send_ve, recv_ve, send_ce, recv_ce, send_w, recv_w, local,
):
    iv = lax.axis_index("val")
    ic = lax.axis_index("cond")
    vb, points = val.shape
    cb = cond.shape[0]
    rows = NW // nv
    planes = points // NG

    barrier = pltpu.get_barrier_semaphore()
    for d in range(nc - 1, 0, -1):
        pl.semaphore_signal(barrier, inc=1, device_id={"cond": partner(ic, d, nc)}, device_id_type=MESH)
    for d in range(1, nv):
        pl.semaphore_signal(barrier, inc=1, device_id={"val": partner(iv, d, nv)}, device_id_type=MESH)

    wave_copy = pltpu.make_async_copy(wave, own_wave, local.at[0])
    own_copies = [
        pltpu.make_async_copy(val, gath_v.at[iv], local.at[1]),
        pltpu.make_async_copy(val_energy, gath_ve.at[iv], local.at[2]),
        pltpu.make_async_copy(cond, gath_c.at[ic], local.at[3]),
        pltpu.make_async_copy(cond_energy, gath_ce.at[ic], local.at[4]),
    ]
    wave_copy.start()
    for copy in own_copies:
        copy.start()
    pl.semaphore_wait(barrier, nc - 1 + nv - 1)

    def window_copy(d):
        return pltpu.make_async_remote_copy(
            src_ref=wave.at[pl.ds(0, 1)], dst_ref=window,
            send_sem=send_w.at[d - 1], recv_sem=recv_w,
            device_id={"cond": partner(ic, d, nc)}, device_id_type=MESH,
        )

    own_window = pltpu.make_async_copy(wave.at[pl.ds(0, 1)], window, local.at[5])

    @pl.when(ic == 0)
    def _():
        for d in range(nc - 1, 0, -1):
            window_copy(d).start()
        own_window.start()

    def exchange(axis, position, size, d, at, src, dst, send, recv):
        return pltpu.make_async_remote_copy(
            src_ref=src, dst_ref=dst.at[at],
            send_sem=send.at[d - 1], recv_sem=recv.at[d - 1],
            device_id={axis: partner(position, d, size)}, device_id_type=MESH,
        )

    def val_copies(d, at):
        return [
            exchange("val", iv, nv, d, at, val, gath_v, send_v, recv_v),
            exchange("val", iv, nv, d, at, val_energy, gath_ve, send_ve, recv_ve),
        ]

    def cond_copies(d, at):
        return [
            exchange("cond", ic, nc, d, at, cond, gath_c, send_c, recv_c),
            exchange("cond", ic, nc, d, at, cond_energy, gath_ce, send_ce, recv_ce),
        ]

    for d in range(nc - 1, 0, -1):
        for copy in cond_copies(d, ic):
            copy.start()
    for d in range(1, nv):
        for copy in val_copies(d, iv):
            copy.start()

    wave_copy.wait()

    for block in range(own_wave.shape[0]):
        cos_x, sin_x, cos_p, sin_p = factors(own_wave[pl.ds(block, 1), :], points, 0.0)
        lanes = pl.ds(block * LANES, LANES)
        for plane in range(planes):
            at = pl.ds(plane * NG, NG)
            c, s = cos_p[plane:plane + 1, :], sin_p[plane:plane + 1, :]
            cos_rows[at, lanes] = (cos_x * c - sin_x * s).astype(jnp.bfloat16)
            sin_rows[at, lanes] = (sin_x * c + cos_x * s).astype(jnp.bfloat16)

    for copy in own_copies:
        copy.wait()
    for d in range(1, nv):
        for copy in val_copies(d, source(iv, d, nv)):
            copy.wait_recv()

    count = group * cb
    height = nv * vb * count
    eye = lax.broadcasted_iota(jnp.int32, (cb, cb), 0) == lax.broadcasted_iota(jnp.int32, (cb, cb), 1)

    def fill(first):
        slot = first // group % slots
        orbitals, energies = [], []
        for d in range(first, first + group):
            at = source(ic, d, nc) if d else ic
            if d:
                for copy in cond_copies(d, at):
                    copy.wait_recv()
            orbitals.append(gath_c[at].astype(jnp.float32))
            row = jnp.broadcast_to(gath_ce[at].astype(jnp.float32), (cb, cb))
            column = jnp.sum(jnp.where(eye, row, 0.0), axis=1, keepdims=True)
            energies.append(jnp.broadcast_to(column, (cb, LANES)))
        orbitals = jnp.concatenate(orbitals, axis=0)

        def one_block(b, carry):
            block = gath_v[b].astype(jnp.float32)
            for v in range(vb):
                at = pl.ds(pl.multiple_of((b * vb + v) * count, count), count)
                dens[slot, at, :] = (orbitals * block[v:v + 1, :]).astype(jnp.bfloat16)
            return carry

        lax.fori_loop(0, nv, one_block, 0, unroll=nv <= 4)
        return jnp.concatenate(energies, axis=0)

    def use(first, energies):
        slot = first // group % slots
        weights = []
        for b in range(nv):
            block = gath_ve[b].astype(jnp.float32)
            for v in range(vb):
                own = jnp.broadcast_to(block[:, v:v + 1], (1, LANES))
                weights.append(1.0 / (energies - own))
        weighted = dot(dens[slot], window_table[...]) * jnp.concatenate(weights, axis=0)
        update = dot(split(jnp.transpose(weighted)[0:2 * rows]), dens[slot])
        update = update[0:2 * rows] + update[2 * rows:4 * rows]
        totals[...] = update if first == 0 else totals[...] + update

    ahead = min(2, slots, nc // group)
    energies = {}
    for step in range(ahead):
        energies[step] = fill(step * group)

    @pl.when(ic == 0)
    def _():
        own_window.wait()

    @pl.when(ic != 0)
    def _():
        window_copy(1).wait_recv()

    spread = jnp.broadcast_to(window[...], (8, LANES))
    first = pltpu.roll(spread, lax.rem(NW - iv * rows, NW), 1)
    lane = lax.broadcasted_iota(jnp.int32, (8, LANES), 1)
    index = jnp.where(lane < rows, first, pltpu.roll(first, rows, 1))[0:1, :]
    shift = jnp.where(lane < rows, 0.0, 3 * NG / 4)[0:1, :]
    cos_x, sin_x, cos_p, sin_p = factors(index, points, shift)
    for plane in range(planes):
        c, s = cos_p[plane:plane + 1, :], sin_p[plane:plane + 1, :]
        window_table[pl.ds(plane * NG, NG), :] = (cos_x * c - sin_x * s).astype(jnp.bfloat16)

    for step in range(nc // group):
        if step >= ahead:
            energies[step] = fill(step * group)
        use(step * group, energies.pop(step))

    cos_total = totals[0:rows, :]
    sin_total = totals[rows:2 * rows, :]
    by_cos = split(jnp.concatenate([cos_total, -sin_total], axis=0))
    by_sin = split(jnp.concatenate([sin_total, cos_total], axis=0))
    both = dot(by_cos, cos_rows[...]) + dot(by_sin, sin_rows[...])
    out[...] = both[0:2 * rows] + both[2 * rows:4 * rows]

    @pl.when(ic == 0)
    def _():
        for d in range(1, nc):
            window_copy(d).wait_send()

    for d in range(1, nc):
        for copy in cond_copies(d, ic):
            copy.wait_send()
    for d in range(1, nv):
        for copy in val_copies(d, iv):
            copy.wait_send()


def per_device(val_orbitals, cond_orbitals, val_energy, cond_energy, wave_index):
    nv, nc = lax.axis_size("val"), lax.axis_size("cond")
    vb, points = val_orbitals.shape
    cb = cond_orbitals.shape[0]
    count = wave_index.shape[0]
    rows = NW // nv
    group = 2 if nc % 2 == 0 else 1
    slots = min(4, nc // group)
    bf16, f32 = jnp.bfloat16, jnp.float32
    dma = pltpu.SemaphoreType.DMA
    out = pl.pallas_call(
        functools.partial(kernel, nv, nc, group, slots),
        out_shape=jax.ShapeDtypeStruct((2 * rows, count), f32),
        in_specs=[pl.BlockSpec(memory_space=pltpu.HBM)] * 5,
        out_specs=pl.BlockSpec(memory_space=pltpu.VMEM),
        scratch_shapes=[
            pltpu.VMEM((nv, vb, points), bf16),
            pltpu.VMEM((nc, cb, points), bf16),
            pltpu.VMEM((nv, 1, vb), bf16),
            pltpu.VMEM((nc, 1, cb), bf16),
            pltpu.VMEM((count // LANES, LANES), jnp.int32),
            pltpu.VMEM((1, LANES), jnp.int32),
            pltpu.VMEM((points, count), bf16),
            pltpu.VMEM((points, count), bf16),
            pltpu.VMEM((points, LANES), bf16),
            pltpu.VMEM((slots, nv * vb * group * cb, points), bf16),
            pltpu.VMEM((2 * rows, points), f32),
            dma((nv - 1,)), dma((nv - 1,)), dma((nc - 1,)), dma((nc - 1,)),
            dma((nv - 1,)), dma((nv - 1,)), dma((nc - 1,)), dma((nc - 1,)),
            dma((nc - 1,)), dma, dma((6,)),
        ],
        compiler_params=pltpu.CompilerParams(
            collective_id=0, has_side_effects=True, vmem_limit_bytes=VMEM_LIMIT
        ),
    )(*[
        pltpu.with_memory_space_constraint(value, pltpu.HBM)
        for value in (
            val_orbitals, cond_orbitals, val_energy.reshape(1, vb), cond_energy.reshape(1, cb),
            wave_index.reshape(count // LANES, LANES),
        )
    ])
    factor = -4.0 / math.sqrt(nv * vb * nc * cb)
    return factor * out[0:rows], factor * out[rows:2 * rows]


def solution(mesh):
    return jax.shard_map(
        per_device,
        mesh=mesh,
        in_specs=(P("val", None), P("cond", None), P("val"), P("cond"), P("cond")),
        out_specs=(P("val", "cond"), P("val", "cond")),
        check_vma=False,
    )
```

```python
import functools
import math

import jax
import jax.numpy as jnp
from jax import lax
from jax.experimental import pallas as pl
from jax.experimental.pallas import tpu as pltpu
from jax.sharding import PartitionSpec as P

NG = 96
NW = 128
SLAB_Y = 4
LANES = 128
VMEM_LIMIT = 24 * 1024 * 1024
MESH = pl.DeviceIdType.MESH


def modulo(value, period):
    return value - period * jnp.floor((value + 0.5) * (1.0 / period))


def cos_turns(turns):
    angle = (turns - NG / 2) * (math.pi / NG)
    square = angle * angle
    series = 1.0
    for order in (10, 8, 6, 4, 2):
        series = 1.0 - square * series * (1.0 / (order * (order + 1)))
    sine = angle * series
    return 2.0 * sine * sine - 1.0


def wave_parts(index):
    flat = index.astype(jnp.float32)
    wave_x = jnp.floor((flat + 0.5) * (1.0 / (NG * NG)))
    rest = flat - wave_x * (NG * NG)
    wave_y = jnp.floor((rest + 0.5) * (1.0 / NG))
    return wave_x, wave_y, rest - wave_y * NG


def factors(index, points, shift):
    wave_x, wave_y, wave_z = wave_parts(index)
    planes = points // NG
    along_x = lax.broadcasted_iota(jnp.int32, (NG, LANES), 0).astype(jnp.float32)
    plane = lax.broadcasted_iota(jnp.int32, (planes, LANES), 0).astype(jnp.float32)
    along_z = jnp.floor((plane + 0.5) * (1.0 / SLAB_Y))
    along_y = plane - along_z * SLAB_Y
    turns_x = modulo(along_x * wave_x, NG)
    turns_yz = modulo(along_y * wave_y + along_z * wave_z + shift, NG)
    quarter = 3 * NG // 4
    return (
        cos_turns(turns_x),
        cos_turns(modulo(turns_x + quarter, NG)),
        cos_turns(turns_yz),
        cos_turns(modulo(turns_yz + quarter, NG)),
    )


def split(value):
    high = value.astype(jnp.bfloat16)
    low = (value - high.astype(jnp.float32)).astype(jnp.bfloat16)
    return jnp.concatenate([high, low], axis=0)


def dot(left, right):
    return jnp.dot(left, right, preferred_element_type=jnp.float32)


def partner(position, offset, size):
    if size & (size - 1):
        return lax.rem(position + offset, size)
    bit = 1
    while bit < size:
        if offset & bit:
            position = position + bit - 2 * bit * lax.rem(position // bit, 2)
        bit *= 2
    return position


def source(position, offset, size):
    if size & (size - 1):
        return lax.rem(position + size - offset, size)
    return partner(position, offset, size)


def kernel(
    nv, nc, group, slots,
    val, cond, val_energy, cond_energy, wave, out,
    gath_v, gath_c, gath_ve, gath_ce, own_wave, window, cos_rows, sin_rows, window_table, dens, totals,
    send_v, recv_v, send_c, recv_c, send_ve, recv_ve, send_ce, recv_ce, send_w, recv_w, local,
):
    iv = lax.axis_index("val")
    ic = lax.axis_index("cond")
    vb, points = val.shape
    cb = cond.shape[0]
    rows = NW // nv
    planes = points // NG

    barrier = pltpu.get_barrier_semaphore()
    for d in range(nc - 1, 0, -1):
        pl.semaphore_signal(barrier, inc=1, device_id={"cond": partner(ic, d, nc)}, device_id_type=MESH)
    for d in range(1, nv):
        pl.semaphore_signal(barrier, inc=1, device_id={"val": partner(iv, d, nv)}, device_id_type=MESH)

    wave_copy = pltpu.make_async_copy(wave, own_wave, local.at[0])
    own_copies = [
        pltpu.make_async_copy(val, gath_v.at[iv], local.at[1]),
        pltpu.make_async_copy(val_energy, gath_ve.at[iv], local.at[2]),
        pltpu.make_async_copy(cond, gath_c.at[ic], local.at[3]),
        pltpu.make_async_copy(cond_energy, gath_ce.at[ic], local.at[4]),
    ]
    wave_copy.start()
    for copy in own_copies:
        copy.start()
    wave_copy.wait()
    for copy in own_copies:
        copy.wait()
    pl.semaphore_wait(barrier, nc - 1 + nv - 1)

    def window_copy(d):
        return pltpu.make_async_remote_copy(
            src_ref=own_wave.at[pl.ds(0, 1)], dst_ref=window,
            send_sem=send_w.at[d - 1], recv_sem=recv_w,
            device_id={"cond": partner(ic, d, nc)}, device_id_type=MESH,
        )

    own_window = pltpu.make_async_copy(wave.at[pl.ds(0, 1)], window, local.at[5])

    @pl.when(ic == 0)
    def _():
        for d in range(nc - 1, 0, -1):
            window_copy(d).start()
        own_window.start()

    def exchange(axis, position, size, d, at, src, dst, send, recv):
        return pltpu.make_async_remote_copy(
            src_ref=src, dst_ref=dst.at[at],
            send_sem=send.at[d - 1], recv_sem=recv.at[d - 1],
            device_id={axis: partner(position, d, size)}, device_id_type=MESH,
        )

    def val_copies(d, at):
        return [
            exchange("val", iv, nv, d, at, gath_v.at[iv], gath_v, send_v, recv_v),
            exchange("val", iv, nv, d, at, gath_ve.at[iv], gath_ve, send_ve, recv_ve),
        ]

    def cond_copies(d, at):
        return [
            exchange("cond", ic, nc, d, at, gath_c.at[ic], gath_c, send_c, recv_c),
            exchange("cond", ic, nc, d, at, gath_ce.at[ic], gath_ce, send_ce, recv_ce),
        ]

    for d in range(nc - 1, 0, -1):
        for copy in cond_copies(d, ic):
            copy.start()
    for d in range(1, nv):
        for copy in val_copies(d, iv):
            copy.start()

    for block in range(own_wave.shape[0]):
        cos_x, sin_x, cos_p, sin_p = factors(own_wave[pl.ds(block, 1), :], points, 0.0)
        lanes = pl.ds(block * LANES, LANES)
        for plane in range(planes):
            at = pl.ds(plane * NG, NG)
            c, s = cos_p[plane:plane + 1, :], sin_p[plane:plane + 1, :]
            cos_rows[at, lanes] = (cos_x * c - sin_x * s).astype(jnp.bfloat16)
            sin_rows[at, lanes] = (sin_x * c + cos_x * s).astype(jnp.bfloat16)

    for d in range(1, nv):
        for copy in val_copies(d, source(iv, d, nv)):
            copy.wait_recv()

    count = group * cb
    height = nv * vb * count
    eye = lax.broadcasted_iota(jnp.int32, (cb, cb), 0) == lax.broadcasted_iota(jnp.int32, (cb, cb), 1)

    def fill(first):
        slot = first // group % slots
        orbitals, energies = [], []
        for d in range(first, first + group):
            at = source(ic, d, nc) if d else ic
            if d:
                for copy in cond_copies(d, at):
                    copy.wait_recv()
            orbitals.append(gath_c[at].astype(jnp.float32))
            row = jnp.broadcast_to(gath_ce[at].astype(jnp.float32), (cb, cb))
            column = jnp.sum(jnp.where(eye, row, 0.0), axis=1, keepdims=True)
            energies.append(jnp.broadcast_to(column, (cb, LANES)))
        orbitals = jnp.concatenate(orbitals, axis=0)

        def one_block(b, carry):
            block = gath_v[b].astype(jnp.float32)
            for v in range(vb):
                at = pl.ds(pl.multiple_of((b * vb + v) * count, count), count)
                dens[slot, at, :] = (orbitals * block[v:v + 1, :]).astype(jnp.bfloat16)
            return carry

        lax.fori_loop(0, nv, one_block, 0, unroll=nv <= 4)
        return jnp.concatenate(energies, axis=0)

    def use(first, energies):
        slot = first // group % slots
        weights = []
        for b in range(nv):
            block = gath_ve[b].astype(jnp.float32)
            for v in range(vb):
                own = jnp.broadcast_to(block[:, v:v + 1], (1, LANES))
                weights.append(1.0 / (energies - own))
        weighted = dot(dens[slot], window_table[...]) * jnp.concatenate(weights, axis=0)
        update = dot(split(jnp.transpose(weighted)[0:2 * rows]), dens[slot])
        update = update[0:2 * rows] + update[2 * rows:4 * rows]
        totals[...] = update if first == 0 else totals[...] + update

    ahead = min(2, slots, nc // group)
    energies = {}
    for step in range(ahead):
        energies[step] = fill(step * group)

    @pl.when(ic == 0)
    def _():
        own_window.wait()

    @pl.when(ic != 0)
    def _():
        window_copy(1).wait_recv()

    spread = jnp.broadcast_to(window[...], (8, LANES))
    first = pltpu.roll(spread, lax.rem(NW - iv * rows, NW), 1)
    lane = lax.broadcasted_iota(jnp.int32, (8, LANES), 1)
    index = jnp.where(lane < rows, first, pltpu.roll(first, rows, 1))[0:1, :]
    shift = jnp.where(lane < rows, 0.0, 3 * NG / 4)[0:1, :]
    cos_x, sin_x, cos_p, sin_p = factors(index, points, shift)
    for plane in range(planes):
        c, s = cos_p[plane:plane + 1, :], sin_p[plane:plane + 1, :]
        window_table[pl.ds(plane * NG, NG), :] = (cos_x * c - sin_x * s).astype(jnp.bfloat16)

    for step in range(nc // group):
        if step >= ahead:
            energies[step] = fill(step * group)
        use(step * group, energies.pop(step))

    cos_total = totals[0:rows, :]
    sin_total = totals[rows:2 * rows, :]
    by_cos = split(jnp.concatenate([cos_total, -sin_total], axis=0))
    by_sin = split(jnp.concatenate([sin_total, cos_total], axis=0))
    both = dot(by_cos, cos_rows[...]) + dot(by_sin, sin_rows[...])
    out[...] = both[0:2 * rows] + both[2 * rows:4 * rows]

    @pl.when(ic == 0)
    def _():
        for d in range(1, nc):
            window_copy(d).wait_send()

    for d in range(1, nc):
        for copy in cond_copies(d, ic):
            copy.wait_send()
    for d in range(1, nv):
        for copy in val_copies(d, iv):
            copy.wait_send()


def per_device(val_orbitals, cond_orbitals, val_energy, cond_energy, wave_index):
    nv, nc = lax.axis_size("val"), lax.axis_size("cond")
    vb, points = val_orbitals.shape
    cb = cond_orbitals.shape[0]
    count = wave_index.shape[0]
    rows = NW // nv
    group = 2 if nc % 2 == 0 else 1
    slots = min(4, nc // group)
    bf16, f32 = jnp.bfloat16, jnp.float32
    dma = pltpu.SemaphoreType.DMA
    out = pl.pallas_call(
        functools.partial(kernel, nv, nc, group, slots),
        out_shape=jax.ShapeDtypeStruct((2 * rows, count), f32),
        in_specs=[pl.BlockSpec(memory_space=pltpu.HBM)] * 5,
        out_specs=pl.BlockSpec(memory_space=pltpu.VMEM),
        scratch_shapes=[
            pltpu.VMEM((nv, vb, points), bf16),
            pltpu.VMEM((nc, cb, points), bf16),
            pltpu.VMEM((nv, 1, vb), bf16),
            pltpu.VMEM((nc, 1, cb), bf16),
            pltpu.VMEM((count // LANES, LANES), jnp.int32),
            pltpu.VMEM((1, LANES), jnp.int32),
            pltpu.VMEM((points, count), bf16),
            pltpu.VMEM((points, count), bf16),
            pltpu.VMEM((points, LANES), bf16),
            pltpu.VMEM((slots, nv * vb * group * cb, points), bf16),
            pltpu.VMEM((2 * rows, points), f32),
            dma((nv - 1,)), dma((nv - 1,)), dma((nc - 1,)), dma((nc - 1,)),
            dma((nv - 1,)), dma((nv - 1,)), dma((nc - 1,)), dma((nc - 1,)),
            dma((nc - 1,)), dma, dma((6,)),
        ],
        compiler_params=pltpu.CompilerParams(
            collective_id=0, has_side_effects=True, vmem_limit_bytes=VMEM_LIMIT
        ),
    )(*[
        pltpu.with_memory_space_constraint(value, pltpu.HBM)
        for value in (
            val_orbitals, cond_orbitals, val_energy.reshape(1, vb), cond_energy.reshape(1, cb),
            wave_index.reshape(count // LANES, LANES),
        )
    ])
    factor = -4.0 / math.sqrt(nv * vb * nc * cb)
    return factor * out[0:rows], factor * out[rows:2 * rows]


def solution(mesh):
    return jax.shard_map(
        per_device,
        mesh=mesh,
        in_specs=(P("val", None), P("cond", None), P("val"), P("cond"), P("cond")),
        out_specs=(P("val", "cond"), P("val", "cond")),
        check_vma=False,
    )
```

```python
import functools
import math

import jax
import jax.numpy as jnp
from jax import lax
from jax.experimental import pallas as pl
from jax.experimental.pallas import tpu as pltpu
from jax.sharding import PartitionSpec as P

NG = 96
NW = 128
SLAB_Y = 4
LANES = 128
VMEM_LIMIT = 24 * 1024 * 1024
MESH = pl.DeviceIdType.MESH


def modulo(value, period):
    return value - period * jnp.floor((value + 0.5) * (1.0 / period))


def cos_turns(turns):
    angle = (turns - NG / 2) * (math.pi / NG)
    square = angle * angle
    series = 1.0
    for order in (10, 8, 6, 4, 2):
        series = 1.0 - square * series * (1.0 / (order * (order + 1)))
    sine = angle * series
    return 2.0 * sine * sine - 1.0


def wave_parts(index):
    flat = index.astype(jnp.float32)
    wave_x = jnp.floor((flat + 0.5) * (1.0 / (NG * NG)))
    rest = flat - wave_x * (NG * NG)
    wave_y = jnp.floor((rest + 0.5) * (1.0 / NG))
    return wave_x, wave_y, rest - wave_y * NG


def factors(index, points, shift):
    wave_x, wave_y, wave_z = wave_parts(index)
    planes = points // NG
    along_x = lax.broadcasted_iota(jnp.int32, (NG, LANES), 0).astype(jnp.float32)
    plane = lax.broadcasted_iota(jnp.int32, (planes, LANES), 0).astype(jnp.float32)
    along_z = jnp.floor((plane + 0.5) * (1.0 / SLAB_Y))
    along_y = plane - along_z * SLAB_Y
    turns_x = modulo(along_x * wave_x, NG)
    turns_yz = modulo(along_y * wave_y + along_z * wave_z + shift, NG)
    quarter = 3 * NG // 4
    return (
        cos_turns(turns_x),
        cos_turns(modulo(turns_x + quarter, NG)),
        cos_turns(turns_yz),
        cos_turns(modulo(turns_yz + quarter, NG)),
    )


def split(value):
    high = value.astype(jnp.bfloat16)
    low = (value - high.astype(jnp.float32)).astype(jnp.bfloat16)
    return jnp.concatenate([high, low], axis=0)


def dot(left, right):
    return jnp.dot(left, right, preferred_element_type=jnp.float32)


def partner(position, offset, size):
    if size & (size - 1):
        return lax.rem(position + offset, size)
    bit = 1
    while bit < size:
        if offset & bit:
            position = position + bit - 2 * bit * lax.rem(position // bit, 2)
        bit *= 2
    return position


def source(position, offset, size):
    if size & (size - 1):
        return lax.rem(position + size - offset, size)
    return partner(position, offset, size)


def kernel(
    nv, nc, group, slots,
    val, cond, val_energy, cond_energy, wave, out,
    gath_v, gath_c, gath_ve, gath_ce, own_wave, window, cos_rows, sin_rows, window_table, dens, totals,
    send_v, recv_v, send_c, recv_c, send_ve, recv_ve, send_ce, recv_ce, send_w, recv_w, local,
):
    iv = lax.axis_index("val")
    ic = lax.axis_index("cond")
    vb, points = val.shape
    cb = cond.shape[0]
    rows = NW // nv
    planes = points // NG

    barrier = pltpu.get_barrier_semaphore()
    for d in range(nc - 1, 0, -1):
        pl.semaphore_signal(barrier, inc=1, device_id={"cond": partner(ic, d, nc)}, device_id_type=MESH)
    for d in range(1, nv):
        pl.semaphore_signal(barrier, inc=1, device_id={"val": partner(iv, d, nv)}, device_id_type=MESH)

    wave_copy = pltpu.make_async_copy(wave, own_wave, local.at[0])
    own_copies = [
        pltpu.make_async_copy(val, gath_v.at[iv], local.at[1]),
        pltpu.make_async_copy(val_energy, gath_ve.at[iv], local.at[2]),
        pltpu.make_async_copy(cond, gath_c.at[ic], local.at[3]),
        pltpu.make_async_copy(cond_energy, gath_ce.at[ic], local.at[4]),
    ]
    wave_copy.start()
    for copy in own_copies:
        copy.start()
    wave_copy.wait()
    for copy in own_copies:
        copy.wait()
    pl.semaphore_wait(barrier, nc - 1 + nv - 1)

    def window_copy(d):
        return pltpu.make_async_remote_copy(
            src_ref=own_wave.at[pl.ds(0, 1)], dst_ref=window,
            send_sem=send_w.at[d - 1], recv_sem=recv_w,
            device_id={"cond": partner(ic, d, nc)}, device_id_type=MESH,
        )

    own_window = pltpu.make_async_copy(wave.at[pl.ds(0, 1)], window, local.at[5])

    @pl.when(ic == 0)
    def _():
        for d in range(nc - 1, 0, -1):
            window_copy(d).start()
        own_window.start()

    def exchange(axis, position, size, d, at, src, dst, send, recv):
        return pltpu.make_async_remote_copy(
            src_ref=src, dst_ref=dst.at[at],
            send_sem=send.at[d - 1], recv_sem=recv.at[d - 1],
            device_id={axis: partner(position, d, size)}, device_id_type=MESH,
        )

    def val_copies(d, at):
        return [
            exchange("val", iv, nv, d, at, gath_v.at[iv], gath_v, send_v, recv_v),
            exchange("val", iv, nv, d, at, gath_ve.at[iv], gath_ve, send_ve, recv_ve),
        ]

    def cond_copies(d, at):
        return [
            exchange("cond", ic, nc, d, at, gath_c.at[ic], gath_c, send_c, recv_c),
            exchange("cond", ic, nc, d, at, gath_ce.at[ic], gath_ce, send_ce, recv_ce),
        ]

    for d in range(nc - 1, 0, -1):
        cond_copies(d, ic)[1].start()
    for d in range(nc - 1, 0, -1):
        cond_copies(d, ic)[0].start()
    for d in range(1, nv):
        for copy in val_copies(d, iv):
            copy.start()

    for block in range(own_wave.shape[0]):
        cos_x, sin_x, cos_p, sin_p = factors(own_wave[pl.ds(block, 1), :], points, 0.0)
        lanes = pl.ds(block * LANES, LANES)
        for plane in range(planes):
            at = pl.ds(plane * NG, NG)
            c, s = cos_p[plane:plane + 1, :], sin_p[plane:plane + 1, :]
            cos_rows[at, lanes] = (cos_x * c - sin_x * s).astype(jnp.bfloat16)
            sin_rows[at, lanes] = (sin_x * c + cos_x * s).astype(jnp.bfloat16)

    for d in range(1, nv):
        for copy in val_copies(d, source(iv, d, nv)):
            copy.wait_recv()

    count = group * cb
    height = nv * vb * count
    eye = lax.broadcasted_iota(jnp.int32, (cb, cb), 0) == lax.broadcasted_iota(jnp.int32, (cb, cb), 1)

    def fill(first):
        slot = first // group % slots
        orbitals, energies, weights = [], [], []
        places = [source(ic, d, nc) if d else ic for d in range(first, first + group)]
        for d, at in zip(range(first, first + group), places):
            if d:
                cond_copies(d, at)[1].wait_recv()
            row = jnp.broadcast_to(gath_ce[at].astype(jnp.float32), (cb, cb))
            column = jnp.sum(jnp.where(eye, row, 0.0), axis=1, keepdims=True)
            energies.append(jnp.broadcast_to(column, (cb, LANES)))
        energies = jnp.concatenate(energies, axis=0)
        for b in range(nv):
            block = gath_ve[b].astype(jnp.float32)
            for v in range(vb):
                own = jnp.broadcast_to(block[:, v:v + 1], (1, LANES))
                weights.append(1.0 / (energies - own))
        for d, at in zip(range(first, first + group), places):
            if d:
                cond_copies(d, at)[0].wait_recv()
            orbitals.append(gath_c[at].astype(jnp.float32))
        orbitals = jnp.concatenate(orbitals, axis=0)

        def one_block(b, carry):
            block = gath_v[b].astype(jnp.float32)
            for v in range(vb):
                at = pl.ds(pl.multiple_of((b * vb + v) * count, count), count)
                dens[slot, at, :] = (orbitals * block[v:v + 1, :]).astype(jnp.bfloat16)
            return carry

        lax.fori_loop(0, nv, one_block, 0, unroll=nv <= 4)
        return jnp.concatenate(weights, axis=0)

    def use(first, weights):
        slot = first // group % slots
        weighted = dot(dens[slot], window_table[...]) * weights
        update = dot(split(jnp.transpose(weighted)[0:2 * rows]), dens[slot])
        update = update[0:2 * rows] + update[2 * rows:4 * rows]
        totals[...] = update if first == 0 else totals[...] + update

    ahead = min(2, slots, nc // group)
    weights = {}
    for step in range(ahead):
        weights[step] = fill(step * group)

    @pl.when(ic == 0)
    def _():
        own_window.wait()

    @pl.when(ic != 0)
    def _():
        window_copy(1).wait_recv()

    spread = jnp.broadcast_to(window[...], (8, LANES))
    first = pltpu.roll(spread, lax.rem(NW - iv * rows, NW), 1)
    lane = lax.broadcasted_iota(jnp.int32, (8, LANES), 1)
    index = jnp.where(lane < rows, first, pltpu.roll(first, rows, 1))[0:1, :]
    shift = jnp.where(lane < rows, 0.0, 3 * NG / 4)[0:1, :]
    cos_x, sin_x, cos_p, sin_p = factors(index, points, shift)
    for plane in range(planes):
        c, s = cos_p[plane:plane + 1, :], sin_p[plane:plane + 1, :]
        window_table[pl.ds(plane * NG, NG), :] = (cos_x * c - sin_x * s).astype(jnp.bfloat16)

    for step in range(nc // group):
        if step >= ahead:
            weights[step] = fill(step * group)
        use(step * group, weights.pop(step))

    cos_total = totals[0:rows, :]
    sin_total = totals[rows:2 * rows, :]
    by_cos = split(jnp.concatenate([cos_total, -sin_total], axis=0))
    by_sin = split(jnp.concatenate([sin_total, cos_total], axis=0))
    both = dot(by_cos, cos_rows[...]) + dot(by_sin, sin_rows[...])
    out[...] = both[0:2 * rows] + both[2 * rows:4 * rows]

    @pl.when(ic == 0)
    def _():
        for d in range(1, nc):
            window_copy(d).wait_send()

    for d in range(1, nc):
        for copy in cond_copies(d, ic):
            copy.wait_send()
    for d in range(1, nv):
        for copy in val_copies(d, iv):
            copy.wait_send()


def per_device(val_orbitals, cond_orbitals, val_energy, cond_energy, wave_index):
    nv, nc = lax.axis_size("val"), lax.axis_size("cond")
    vb, points = val_orbitals.shape
    cb = cond_orbitals.shape[0]
    count = wave_index.shape[0]
    rows = NW // nv
    group = 2 if nc % 2 == 0 else 1
    slots = min(4, nc // group)
    bf16, f32 = jnp.bfloat16, jnp.float32
    dma = pltpu.SemaphoreType.DMA
    out = pl.pallas_call(
        functools.partial(kernel, nv, nc, group, slots),
        out_shape=jax.ShapeDtypeStruct((2 * rows, count), f32),
        in_specs=[pl.BlockSpec(memory_space=pltpu.HBM)] * 5,
        out_specs=pl.BlockSpec(memory_space=pltpu.VMEM),
        scratch_shapes=[
            pltpu.VMEM((nv, vb, points), bf16),
            pltpu.VMEM((nc, cb, points), bf16),
            pltpu.VMEM((nv, 1, vb), bf16),
            pltpu.VMEM((nc, 1, cb), bf16),
            pltpu.VMEM((count // LANES, LANES), jnp.int32),
            pltpu.VMEM((1, LANES), jnp.int32),
            pltpu.VMEM((points, count), bf16),
            pltpu.VMEM((points, count), bf16),
            pltpu.VMEM((points, LANES), bf16),
            pltpu.VMEM((slots, nv * vb * group * cb, points), bf16),
            pltpu.VMEM((2 * rows, points), f32),
            dma((nv - 1,)), dma((nv - 1,)), dma((nc - 1,)), dma((nc - 1,)),
            dma((nv - 1,)), dma((nv - 1,)), dma((nc - 1,)), dma((nc - 1,)),
            dma((nc - 1,)), dma, dma((6,)),
        ],
        compiler_params=pltpu.CompilerParams(
            collective_id=0, has_side_effects=True, vmem_limit_bytes=VMEM_LIMIT
        ),
    )(*[
        pltpu.with_memory_space_constraint(value, pltpu.HBM)
        for value in (
            val_orbitals, cond_orbitals, val_energy.reshape(1, vb), cond_energy.reshape(1, cb),
            wave_index.reshape(count // LANES, LANES),
        )
    ])
    factor = -4.0 / math.sqrt(nv * vb * nc * cb)
    return factor * out[0:rows], factor * out[rows:2 * rows]


def solution(mesh):
    return jax.shard_map(
        per_device,
        mesh=mesh,
        in_specs=(P("val", None), P("cond", None), P("val"), P("cond"), P("cond")),
        out_specs=(P("val", "cond"), P("val", "cond")),
        check_vma=False,
    )
```
